32 devices in a mesh: parts: 2 (over y), row: 4 (over z), col: 4 (over x, core).
Axes of the slice: x: 2, y: 2, z: 4, core: 2. Of those that a mesh axis runs over, the one named last changes fastest.
Arguments:
- amplitudes: bfloat16 [8, 100, 512, 512], P('parts', 'col', 'row'), parts along dimension 0, may hold values from -12 to 12
- integrals: bfloat16 [200, 512, 512], P(('parts', 'col'), 'row'), parts along dimension 0, may hold values from -0.109375 to 0.109375
- occ_irrep: int32 [200], P('parts'), parts along dimension 0, may hold values from 0 to 7, as said below
- vir_irrep: int32 [1024], P('parts'), parts along dimension 0, may hold values from 0 to 7, as said below
- screen: int32 [200, 8], P('parts'), parts along dimension 0, may hold values 0 or 1
- occ_energy: float32 [200], P('parts'), parts along dimension 0, may hold values from -1 to -0.3
- vir_energy: float32 [1024], P('parts'), parts along dimension 0, may hold values from 0.1 to 1
Outputs:
- update: float32 [512, 8, 512], P('row', 'parts', 'col'), parts along dimension 1
The draws below stay inside these ranges and needn't reach their ends.
There are 2 independent parts, one for each index of `parts`. The reference program is written for one: setup_inputs(seed, part) draws one part's arguments, and reference() takes and returns one part's arrays. A program takes and returns all parts, laid end to end along the dimension named above; each array names one. Nothing has to cross between parts.
Inputs may be any that keep to these rules, and one draw needn't show every extreme that they name: `occ_irrep`: the labels never fall from one orbital to the next; the first is 0 and the last is 7. `vir_irrep`: the labels never fall from one orbital to the next and every label from 0 to 7 occurs; exactly one label covers 256 virtual orbitals, every other label fewer.
All inputs are finite; a program needn't handle non-finite values.
Results may differ from the reference program's by a relative error of at most 0.0003.
Values may be sent and summed in bfloat16 or wider, within the bound.
A program may use at most 128 MiB of HBM per device.

```python
import jax
import jax.numpy as jnp
from jax import lax

O = 100
V = 512
NI = 4
VMAX = 256


def sorted_labels(key, length):
    left_key, right_key = jax.random.split(key)
    smaller = jnp.minimum(jax.random.randint(left_key, (length - 2,), 0, 8), jax.random.randint(right_key, (length - 2,), 0, 8))
    bounds = jnp.array([0, 7], dtype=jnp.int32)
    return jnp.sort(jnp.concatenate([bounds, smaller.astype(jnp.int32)]))


def draw_occ_irrep(key, part):
    return sorted_labels(jax.random.fold_in(key, 11), O)


def draw_vir_irrep(key, part):
    label_key, spread_key = jax.random.split(jax.random.fold_in(key, 23))
    largest = jax.random.randint(label_key, (), 0, 8).astype(jnp.int32)
    spare_count = V - VMAX - 7
    picks = jax.random.randint(spread_key, (spare_count,), 0, 7).astype(jnp.int32)
    other_codes = jnp.arange(7, dtype=jnp.int32)
    other_counts = 1 + jnp.sum((picks[:, None] == other_codes[None, :]).astype(jnp.int32), axis=0)
    label_codes = jnp.arange(8, dtype=jnp.int32)
    other_index = label_codes - (label_codes > largest).astype(jnp.int32)
    other_index = jnp.minimum(other_index, 6)
    counts = jnp.where(label_codes == largest, jnp.int32(VMAX), other_counts[other_index])
    edges = jnp.cumsum(counts).astype(jnp.int32)
    positions = jnp.arange(V, dtype=jnp.int32)
    return jnp.sum((positions[:, None] >= edges[None, :]).astype(jnp.int32), axis=1).astype(jnp.int32)


def place_ends(values, own_key, smallest, high):
    place = [jax.random.randint(jax.random.fold_in(own_key, axis), (), 0, length) for axis, length in enumerate(values.shape)]
    widest = values.shape.index(max(values.shape))
    beside = place[:widest] + [(place[widest] + 1) % values.shape[widest]] + place[widest + 1:]
    return values.at[tuple(place)].set(smallest).at[tuple(beside)].set(high)


def spiked(values, rng, source, target, shards_of, factor):
    def block_of(axis_at):
        return (jnp.arange(values.shape[axis_at]) // (values.shape[axis_at] // shards_of)).reshape((-1,) + (1,) * (values.ndim - 1 - axis_at))

    near = jax.random.permutation(rng, shards_of)[block_of(target)]
    second = (block_of(target) + shards_of // 2) % shards_of
    return jnp.where((block_of(source) == near) | (block_of(source) == second), factor * values, values)


def steps_of(key, extent, pieces, smallest, high):
    level = 1.0
    for position, parts in pieces:
        steps = jax.random.uniform(jax.random.fold_in(jax.random.fold_in(key, 6), position), (parts,), jnp.float32, smallest / len(pieces), high / len(pieces))
        level = level * jnp.repeat(jnp.exp(steps), extent[position] // parts).reshape((-1,) + (1,) * (len(extent) - 1 - position))
    return level


def scatter_about(own_key, dims, width, bound, cuts=(), kind=jnp.bfloat16):
    values = width * jax.random.normal(own_key, dims, jnp.float32)
    if cuts:
        values = values * steps_of(own_key, dims, cuts, -0.22, 0.18)
    return jnp.clip(values, -bound, bound).astype(kind)


def heavy_noise(rng, dims, spread, bound, pieces, heavy, held_as=jnp.bfloat16):
    drawn = spread * jax.random.normal(rng, dims, jnp.float32)
    if pieces:
        drawn = drawn * steps_of(rng, dims, pieces, -0.22, 0.18)
    return jnp.clip(spiked(drawn, jax.random.fold_in(rng, 3), *heavy), -bound, bound).astype(held_as)


def setup_inputs(seed: int = 0, part: int = 0) -> dict:
    key_of = jax.random.split(jax.random.key(seed), 8)
    part_keys = jax.random.split(jax.random.fold_in(key_of[7], part), 8)
    amplitudes = scatter_about(part_keys[0], (NI, O, V, V), 2.0, 12.0, ((1, 4), (2, 4)))
    integrals = heavy_noise(part_keys[1], (O, V, V), (O * V // 8) ** -0.5, 0.109375, ((0, 4), (1, 4)), (1, 2, 4, 2.0))
    occ_irrep = draw_occ_irrep(jax.random.fold_in(jax.random.fold_in(key_of[7], part), 71), part)
    vir_irrep = draw_vir_irrep(jax.random.fold_in(jax.random.fold_in(key_of[7], part), 71), part)
    screen = place_ends((jax.random.randint(part_keys[4], (O, 8), 0, 4) < 3).astype(jnp.int32), jax.random.fold_in(part_keys[4], 1), 0, 1)
    occ_energy = jnp.clip(jax.random.uniform(part_keys[5], (O,), jnp.float32, -1.0, -0.3), -1.0, -0.3)
    vir_energy = jnp.clip(jax.random.uniform(part_keys[6], (V,), jnp.float32, 0.1, 1.0), 0.1, 1.0)
    return {"amplitudes": amplitudes, "integrals": integrals, "occ_irrep": occ_irrep, "vir_irrep": vir_irrep, "screen": screen, "occ_energy": occ_energy, "vir_energy": vir_energy}


def parity(first_label, second_label, third_label, fourth_label):
    return jnp.bitwise_xor(jnp.bitwise_xor(first_label, second_label), jnp.bitwise_xor(third_label, fourth_label))


def reference(amplitudes, integrals, occ_irrep, vir_irrep, screen, occ_energy, vir_energy):
    pair_label = occ_irrep[NI]
    irrep_codes = jnp.arange(8, dtype=jnp.int32)
    screen_cols = jnp.sum(screen[:, None, :] * (vir_irrep[None, :, None] == irrep_codes).astype(jnp.int32), axis=2)
    keep_int = (parity(occ_irrep[:, None, None], vir_irrep[None, :, None], pair_label, vir_irrep[None, None, :]) == 0) & (screen_cols[:, :, None] == 1)
    int_kept = jnp.where(keep_int, integrals, jnp.zeros_like(integrals))
    int_wide = int_kept.astype(jnp.float32)

    def one_orbital(inputs):
        amp_block, batch_label = inputs
        keep_amp = parity(batch_label, occ_irrep[:, None, None], vir_irrep[None, :, None], vir_irrep[None, None, :]) == 0
        amp_kept = jnp.where(keep_amp, amp_block, jnp.zeros_like(amp_block))
        return lax.dot_general(int_wide, amp_kept.astype(jnp.float32), (((0, 1), (0, 2)), ((), ())), precision=lax.Precision.HIGHEST)

    cycle_rows = lax.map(one_orbital, (amplitudes, occ_irrep[:NI]))
    cycle_all = jnp.transpose(cycle_rows, (1, 0, 2))
    denominator = occ_energy[:NI][None, :, None] + occ_energy[NI] - vir_energy[None, None, :] - vir_energy[:, None, None]
    return cycle_all / denominator
```

```python
import jax
import jax.numpy as jnp
from jax import lax
from jax.sharding import PartitionSpec as P


def folded_integrals(integrals, occ_local, vir_local, vir_irrep, screen_rows, pair_label):
    half = vir_irrep.shape[0] // 2
    irrep_codes = jnp.arange(8, dtype=jnp.int32)
    screen_local = jnp.sum(
        screen_rows[:, None, :] * (vir_local[None, :, None] == irrep_codes).astype(jnp.int32),
        axis=2,
    )
    wanted = jnp.bitwise_xor(jnp.bitwise_xor(occ_local[:, None], vir_local[None, :]), pair_label)
    wanted = jnp.where(screen_local == 1, wanted, -1)[:, :, None]
    zeros = jnp.zeros((), integrals.dtype)
    low = jnp.where(wanted == vir_irrep[None, None, :half], integrals[:, :, :half], zeros)
    return jnp.where(wanted == vir_irrep[None, None, half:], integrals[:, :, half:], low)


def on_device(amplitudes, integrals, occ_irrep, vir_irrep, screen, occ_energy, vir_energy):
    row_count = lax.axis_size("row")
    column_count = lax.axis_size("col")
    row, col = lax.axis_index("row"), lax.axis_index("col")
    batch_size, occ_share, vir_share, vir_total = amplitudes.shape
    half = vir_total // 2
    vir_columns = vir_total // column_count
    occ_offset = col * occ_share
    occ_local = lax.dynamic_slice_in_dim(occ_irrep, occ_offset, occ_share)
    vir_local = lax.dynamic_slice_in_dim(vir_irrep, row * vir_share, vir_share)
    screen_rows = lax.dynamic_slice_in_dim(screen, occ_offset, occ_share, 0)
    pair_label = occ_irrep[batch_size]

    folded = folded_integrals(
        integrals, occ_local, vir_local, vir_irrep, screen_rows, pair_label
    )
    gathered = lax.all_gather(folded, "row", axis=1, tiled=True)
    shift = jnp.bitwise_xor(occ_irrep[:batch_size, None], occ_local[None, :])
    keep_amp = (
        jnp.bitwise_xor(shift[:, :, None], vir_local[None, None, :])[:, :, :, None]
        == vir_irrep[None, None, None, :]
    )
    amp_kept = jnp.where(keep_amp, amplitudes, jnp.zeros_like(amplitudes))
    partial = lax.dot_general(
        amp_kept, gathered, (((1, 3), (0, 1)), ((), ())), preferred_element_type=jnp.float32
    )

    if row_count == column_count and column_count == 4:
        piece = lax.psum_scatter(partial, "col", scatter_dimension=2, tiled=True)
        routes = []
        for flip in (0, 1):
            pairs = []
            for r in range(row_count):
                for q in range(column_count):
                    target = q // 2 + 2 * ((q + flip) % 2)
                    pairs.append((r * column_count + q, target * column_count + r))
            routes.append(lax.ppermute(piece, ("row", "col"), pairs))
        swap = row // 2 == 1
        first = jnp.where(swap, routes[1], routes[0])
        second = jnp.where(swap, routes[0], routes[1])
        cycle = jnp.concatenate([first, second], axis=2)
    else:
        whole = lax.all_gather(lax.psum(partial, "col"), "row", axis=1, tiled=True)
        cycle = lax.dynamic_slice_in_dim(whole, col * vir_columns, vir_columns, 1)
        cycle = lax.dynamic_slice_in_dim(cycle, (row * vir_share) % half, vir_share, 2)
    cycle = jnp.transpose(cycle, (2, 0, 1))
    col_irrep = lax.dynamic_slice_in_dim(vir_irrep, col * vir_columns, vir_columns)
    kept = (
        jnp.bitwise_xor(occ_irrep[:batch_size, None], pair_label ^ col_irrep[None, :])[None]
        == vir_local[:, None, None]
    )
    cycle = jnp.where(kept, cycle, 0.0)
    energy_cols = lax.dynamic_slice_in_dim(vir_energy, col * vir_columns, vir_columns)
    energy_rows = lax.dynamic_slice_in_dim(vir_energy, row * vir_share, vir_share)
    denominator = (
        occ_energy[:batch_size][None, :, None]
        + occ_energy[batch_size]
        - energy_cols[None, None, :]
        - energy_rows[:, None, None]
    )
    return cycle / denominator


def solution(mesh):
    in_specs = (
        P("parts", "col", "row", None),
        P(("parts", "col"), "row", None),
        P("parts"),
        P("parts"),
        P("parts", None),
        P("parts"),
        P("parts"),
    )
    out_specs = P("row", "parts", "col")
    return jax.shard_map(
        on_device, mesh=mesh, in_specs=in_specs, out_specs=out_specs, check_vma=False
    )
```

```python
import functools

import jax
import jax.numpy as jnp
from jax import lax
from jax.experimental import pallas as pl
from jax.experimental.pallas import tpu as pltpu
from jax.sharding import PartitionSpec as P

LANES = 128
SIDE = 4
PIECES = 5


def folded_integrals(integrals, occ_local, vir_local, vir_irrep, screen_rows, pair_label):
    half = vir_irrep.shape[0] // 2
    irrep_codes = jnp.arange(8, dtype=jnp.int32)
    screen_local = jnp.sum(
        screen_rows[:, None, :] * (vir_local[None, :, None] == irrep_codes).astype(jnp.int32),
        axis=2,
    )
    wanted = jnp.bitwise_xor(jnp.bitwise_xor(occ_local[:, None], vir_local[None, :]), pair_label)
    wanted = jnp.where(screen_local == 1, wanted, -1)[:, :, None]
    zeros = jnp.zeros((), integrals.dtype)
    low = jnp.where(wanted == vir_irrep[None, None, :half], integrals[:, :, :half], zeros)
    return jnp.where(wanted == vir_irrep[None, None, half:], integrals[:, :, half:], low)


def cycle_kernel(
    step,
    occ_ref,
    screen_ref,
    label_rows_ref,
    label_cols_ref,
    int_hbm,
    amp_hbm,
    out_ref,
    raw,
    amp,
    mask,
    one_hot,
    shards,
    total,
    from_cols,
    halves,
    landed,
    raw_sem,
    amp_sem,
    send_sem,
    recv_sem,
    col_send,
    col_recv,
    end_send,
    end_recv,
):
    part, row, col = lax.axis_index("parts"), lax.axis_index("row"), lax.axis_index("col")
    batch_size = amp.shape[1]
    occ_share = raw.shape[0]
    first_k = col * occ_share

    def remote(source, target, send, recv, to_row, to_col):
        return pltpu.make_async_remote_copy(
            src_ref=source,
            dst_ref=target,
            send_sem=send,
            recv_sem=recv,
            device_id=(part, to_row, to_col),
            device_id_type=pl.DeviceIdType.MESH,
        )

    raw_copies = []
    for j in range(PIECES):
        span = pl.ds(j * step, step)
        copy = pltpu.make_async_copy(int_hbm.at[span], raw.at[span], raw_sem.at[j])
        copy.start()
        raw_copies.append(copy)
    amp_copies = []
    for c in range(SIDE):
        copy = pltpu.make_async_copy(
            amp_hbm.at[:, :, :, pl.ds(c * LANES, LANES)], amp.at[c], amp_sem.at[c]
        )
        copy.start()
        amp_copies.append(copy)

    barrier = pltpu.get_barrier_semaphore()
    for ahead_row in range(SIDE):
        for ahead_col in range(SIDE):
            if ahead_row or ahead_col:
                pl.semaphore_signal(
                    barrier,
                    inc=1,
                    device_id=(
                        part,
                        lax.rem(row + ahead_row, SIDE),
                        lax.rem(col + ahead_col, SIDE),
                    ),
                    device_id_type=pl.DeviceIdType.MESH,
                )

    row_label = label_cols_ref[...]
    for c in range(SIDE):
        differ = jnp.bitwise_xor(row_label, label_rows_ref[c : c + 1, :])
        for m in range(8):
            mask[c, m] = jnp.where(differ == m, 1.0, 0.0).astype(mask.dtype)
    for m in range(8):
        one_hot[m] = jnp.where(row_label == m, 1.0, 0.0)
    total[...] = jnp.zeros_like(total)

    def fold(k, carry):
        shift = jnp.bitwise_xor(occ_ref[first_k + k], occ_ref[batch_size])
        screened = jnp.zeros((LANES, LANES), jnp.float32)
        for m in range(8):
            screened += screen_ref[(first_k + k) * 8 + m].astype(jnp.float32) * one_hot[m]
        screened = screened.astype(raw.dtype)
        for h in range(SIDE // 2):
            low = raw[k, :, h * LANES : (h + 1) * LANES] * mask[h, shift]
            g = h + SIDE // 2
            high = raw[k, :, g * LANES : (g + 1) * LANES] * mask[g, shift]
            shards[row, k, :, h * LANES : (h + 1) * LANES] = (low + high) * screened
        return carry

    def hop(distance, j, up):
        way = 0 if up else 1
        owner = row - distance if up else row + distance
        piece = shards.at[owner, pl.ds(j * step, step)]
        return remote(
            piece,
            piece,
            send_sem.at[way, distance, j],
            recv_sem.at[way, distance, j],
            row + 1 if up else row - 1,
            col,
        )

    def arrival(distance, j, up):
        way = 0 if up else 1
        owner = row - distance if up else row + distance
        piece = shards.at[owner, pl.ds(j * step, step)]
        return remote(
            piece,
            piece,
            send_sem.at[way, distance - 1, j],
            recv_sem.at[way, distance - 1, j],
            row - 1 if up else row + 1,
            col,
        )

    def accumulate(owner, j):
        def one(t, carry):
            k = j * step + t
            rows = []
            for i in range(batch_size):
                shift = jnp.bitwise_xor(occ_ref[i], occ_ref[first_k + k])
                rows.append(amp[owner, i, k] * mask[owner, shift])
            total[...] += jnp.dot(
                jnp.concatenate(rows, axis=0),
                shards[owner, k],
                preferred_element_type=jnp.float32,
            )
            return carry

        lax.fori_loop(0, step, one, 0)

    for j in range(PIECES):
        raw_copies[j].wait()
        lax.fori_loop(j * step, (j + 1) * step, fold, 0)
        if j == 0:
            pl.semaphore_wait(barrier, SIDE * SIDE - 1)

        @pl.when(row < SIDE - 1)
        def _():
            hop(0, j, True).start()

        @pl.when(row > 0)
        def _():
            hop(0, j, False).start()

    for copy in amp_copies:
        copy.wait()
    for j in range(PIECES):
        accumulate(row, j)

    for distance in range(1, SIDE):
        for j in range(PIECES):

            @pl.when(row >= distance)
            def _():
                arrival(distance, j, True).wait_recv()
                if distance < SIDE - 1:

                    @pl.when(row < SIDE - 1)
                    def _():
                        hop(distance, j, True).start()

            @pl.when(row + distance < SIDE)
            def _():
                arrival(distance, j, False).wait_recv()
                if distance < SIDE - 1:

                    @pl.when(row > 0)
                    def _():
                        hop(distance, j, False).start()

            @pl.when(row >= distance)
            def _():
                accumulate(row - distance, j)

            @pl.when(row + distance < SIDE)
            def _():
                accumulate(row + distance, j)

    share = total.shape[0] // SIDE
    col_copies = []
    for ahead in range(1, SIDE):
        to_col = lax.rem(col + ahead, SIDE)
        copy = remote(
            total.at[pl.ds(pl.multiple_of(to_col * share, share), share)],
            from_cols.at[ahead - 1],
            col_send.at[ahead - 1],
            col_recv.at[ahead - 1],
            row,
            to_col,
        )
        copy.start()
        col_copies.append(copy)
    summed = total[pl.ds(pl.multiple_of(col * share, share), share), :]
    for ahead in range(1, SIDE):
        col_copies[ahead - 1].wait_recv()
        summed += from_cols[ahead - 1]
    halves[0] = summed[:, :LANES]
    halves[1] = summed[:, LANES:]

    def deliver(ahead):
        to_row = lax.rem(row + ahead, SIDE)
        return remote(
            halves.at[lax.rem(to_row, 2)],
            landed.at[col],
            end_send.at[ahead],
            end_recv.at[col],
            to_row,
            row,
        )

    for ahead in range(1, SIDE):
        deliver(ahead).start()

    @pl.when(row != col)
    def _():
        deliver(0).start()

    @pl.when(row == col)
    def _():
        landed[col] = halves[lax.rem(row, 2)]

    def delivered(i):
        return remote(
            halves.at[0],
            landed.at[i],
            end_send.at[0],
            end_recv.at[i],
            lax.rem(row + 1, SIDE),
            col,
        )

    for i in range(SIDE):

        @pl.when((row != col) | (col != i))
        def _():
            delivered(i).wait_recv()

        out_ref[i] = landed[i]

    for ahead in range(1, SIDE):
        col_copies[ahead - 1].wait_send()
        deliver(ahead).wait_send()

    @pl.when(row != col)
    def _():
        deliver(0).wait_send()

    for distance in range(SIDE - 1):
        for j in range(PIECES):

            @pl.when((row >= distance) & (row < SIDE - 1))
            def _():
                hop(distance, j, True).wait_send()

            @pl.when((row + distance < SIDE) & (row > 0))
            def _():
                hop(distance, j, False).wait_send()


def cycle_blocks(amplitudes, integrals, occ_irrep, vir_irrep, vir_local, screen):
    batch_size, occ_share, vir_share, vir_total = amplitudes.shape
    half = vir_total // 2
    bf16, f32 = jnp.bfloat16, jnp.float32
    step = occ_share // PIECES
    vmem, smem = pltpu.VMEM, pltpu.SMEM
    hops = (2, SIDE - 1, PIECES)
    return pl.pallas_call(
        functools.partial(cycle_kernel, step),
        out_shape=jax.ShapeDtypeStruct((batch_size, LANES, LANES), f32),
        in_specs=[
            pl.BlockSpec(memory_space=smem),
            pl.BlockSpec(memory_space=smem),
            pl.BlockSpec(memory_space=vmem),
            pl.BlockSpec(memory_space=vmem),
            pl.BlockSpec(memory_space=pl.ANY),
            pl.BlockSpec(memory_space=pl.ANY),
        ],
        out_specs=pl.BlockSpec(memory_space=vmem),
        scratch_shapes=[
            vmem((occ_share, vir_share, vir_total), bf16),
            vmem((SIDE, batch_size, occ_share, vir_share, LANES), bf16),
            vmem((SIDE, 8, vir_share, LANES), bf16),
            vmem((8, vir_share, LANES), f32),
            vmem((SIDE, occ_share, vir_share, half), bf16),
            vmem((batch_size * vir_share, half), f32),
            vmem((SIDE - 1, vir_share, half), f32),
            vmem((2, vir_share, LANES), f32),
            vmem((SIDE, vir_share, LANES), f32),
            pltpu.SemaphoreType.DMA((PIECES,)),
            pltpu.SemaphoreType.DMA((SIDE,)),
            pltpu.SemaphoreType.DMA(hops),
            pltpu.SemaphoreType.DMA(hops),
            pltpu.SemaphoreType.DMA((SIDE - 1,)),
            pltpu.SemaphoreType.DMA((SIDE - 1,)),
            pltpu.SemaphoreType.DMA((SIDE,)),
            pltpu.SemaphoreType.DMA((SIDE,)),
        ],
        compiler_params=pltpu.CompilerParams(
            collective_id=0, has_side_effects=True, vmem_limit_bytes=48 * 1024 * 1024
        ),
        name="cycle_blocks",
    )(
        occ_irrep,
        screen.reshape(-1),
        vir_irrep.reshape(SIDE, LANES),
        jnp.broadcast_to(vir_local[:, None], (vir_share, LANES)),
        integrals,
        amplitudes,
    )


def fits_kernel(row_count, column_count, amplitudes):
    batch_size, occ_share, vir_share, vir_total = amplitudes.shape
    return (
        row_count == column_count == batch_size == SIDE
        and vir_share == LANES
        and vir_total == SIDE * LANES
        and occ_share % PIECES == 0
    )


def on_device(amplitudes, integrals, occ_irrep, vir_irrep, screen, occ_energy, vir_energy):
    row_count = lax.axis_size("row")
    column_count = lax.axis_size("col")
    row, col = lax.axis_index("row"), lax.axis_index("col")
    batch_size, occ_share, vir_share, vir_total = amplitudes.shape
    half = vir_total // 2
    vir_columns = vir_total // column_count
    occ_offset = col * occ_share
    occ_local = lax.dynamic_slice_in_dim(occ_irrep, occ_offset, occ_share)
    vir_local = lax.dynamic_slice_in_dim(vir_irrep, row * vir_share, vir_share)
    screen_rows = lax.dynamic_slice_in_dim(screen, occ_offset, occ_share, 0)
    pair_label = occ_irrep[batch_size]

    if fits_kernel(row_count, column_count, amplitudes):
        cycle = cycle_blocks(amplitudes, integrals, occ_irrep, vir_irrep, vir_local, screen)
    else:
        folded = folded_integrals(
            integrals, occ_local, vir_local, vir_irrep, screen_rows, pair_label
        )
        gathered = lax.all_gather(folded, "row", axis=1, tiled=True)
        shift = jnp.bitwise_xor(occ_irrep[:batch_size, None], occ_local[None, :])
        keep_amp = (
            jnp.bitwise_xor(shift[:, :, None], vir_local[None, None, :])[:, :, :, None]
            == vir_irrep[None, None, None, :]
        )
        amp_kept = jnp.where(keep_amp, amplitudes, jnp.zeros_like(amplitudes))
        partial = lax.dot_general(
            amp_kept, gathered, (((1, 3), (0, 1)), ((), ())), preferred_element_type=jnp.float32
        )
        whole = lax.all_gather(lax.psum(partial, "col"), "row", axis=1, tiled=True)
        cycle = lax.dynamic_slice_in_dim(whole, col * vir_columns, vir_columns, 1)
        cycle = lax.dynamic_slice_in_dim(cycle, (row * vir_share) % half, vir_share, 2)
    cycle = jnp.transpose(cycle, (2, 0, 1))
    col_irrep = lax.dynamic_slice_in_dim(vir_irrep, col * vir_columns, vir_columns)
    kept = (
        jnp.bitwise_xor(occ_irrep[:batch_size, None], pair_label ^ col_irrep[None, :])[None]
        == vir_local[:, None, None]
    )
    cycle = jnp.where(kept, cycle, 0.0)
    energy_cols = lax.dynamic_slice_in_dim(vir_energy, col * vir_columns, vir_columns)
    energy_rows = lax.dynamic_slice_in_dim(vir_energy, row * vir_share, vir_share)
    denominator = (
        occ_energy[:batch_size][None, :, None]
        + occ_energy[batch_size]
        - energy_cols[None, None, :]
        - energy_rows[:, None, None]
    )
    return cycle / denominator


def solution(mesh):
    in_specs = (
        P("parts", "col", "row", None),
        P(("parts", "col"), "row", None),
        P("parts"),
        P("parts"),
        P("parts", None),
        P("parts"),
        P("parts"),
    )
    out_specs = P("row", "parts", "col")
    return jax.shard_map(
        on_device, mesh=mesh, in_specs=in_specs, out_specs=out_specs, check_vma=False
    )
```

```python
import functools

import jax
import jax.numpy as jnp
from jax import lax
from jax.experimental import pallas as pl
from jax.experimental.pallas import tpu as pltpu
from jax.sharding import PartitionSpec as P

LANES = 128
SIDE = 4
GIVEN = (4, 3)
OWN = 3
PIECES = len(GIVEN) + OWN


def folded_integrals(integrals, occ_local, vir_local, vir_irrep, screen_rows, pair_label):
    half = vir_irrep.shape[0] // 2
    irrep_codes = jnp.arange(8, dtype=jnp.int32)
    screen_local = jnp.sum(
        screen_rows[:, None, :] * (vir_local[None, :, None] == irrep_codes).astype(jnp.int32),
        axis=2,
    )
    wanted = jnp.bitwise_xor(jnp.bitwise_xor(occ_local[:, None], vir_local[None, :]), pair_label)
    wanted = jnp.where(screen_local == 1, wanted, -1)[:, :, None]
    zeros = jnp.zeros((), integrals.dtype)
    low = jnp.where(wanted == vir_irrep[None, None, :half], integrals[:, :, :half], zeros)
    return jnp.where(wanted == vir_irrep[None, None, half:], integrals[:, :, half:], low)


def cycle_kernel(
    sizes,
    occ_ref,
    screen_ref,
    occ_energy_ref,
    label_rows_ref,
    energy_rows_ref,
    int_hbm,
    amp_hbm,
    out_ref,
    raw,
    amp,
    mask,
    one_hot,
    shards,
    total,
    from_cols,
    halves,
    landed,
    end_mask,
    amp_out,
    amp_in,
    end_total,
    end_cols,
    end_sum,
    from_inner,
    raw_sem,
    amp_sem,
    send_sem,
    recv_sem,
    col_send,
    col_recv,
    end_send,
    end_recv,
    give_send,
    give_recv,
    give_col_send,
    give_col_recv,
    back_send,
    back_recv,
):
    part, row, col = lax.axis_index("parts"), lax.axis_index("row"), lax.axis_index("col")
    batch_size = amp.shape[1]
    occ_share = raw.shape[0]
    first_k = col * occ_share
    is_end = (row == 0) | (row == SIDE - 1)
    is_inner = (row > 0) & (row < SIDE - 1)
    upper = row // (SIDE // 2)
    end_row = upper * (SIDE - 1)
    inner_row = 1 + upper * (SIDE - 3)
    starts = [sum(sizes[:j]) for j in range(PIECES + 1)]

    def span_of(j):
        return pl.ds(starts[j], sizes[j])

    def column_of(ref, which):
        return jnp.broadcast_to(ref[pl.ds(which, 1), :], (LANES, LANES)).T

    def remote(source, target, send, recv, to_row, to_col):
        return pltpu.make_async_remote_copy(
            src_ref=source,
            dst_ref=target,
            send_sem=send,
            recv_sem=recv,
            device_id=(part, to_row, to_col),
            device_id_type=pl.DeviceIdType.MESH,
        )

    raw_copies = []
    for j in range(PIECES):
        span = span_of(j)
        copy = pltpu.make_async_copy(int_hbm.at[span], raw.at[span], raw_sem.at[j])
        copy.start()
        raw_copies.append(copy)
    amp_copies = []
    for c in range(SIDE):
        copy = pltpu.make_async_copy(
            amp_hbm.at[:, :, :, pl.ds(c * LANES, LANES)], amp.at[c], amp_sem.at[c]
        )
        copy.start()
        amp_copies.append(copy)

    barrier = pltpu.get_barrier_semaphore()
    for ahead_row in range(SIDE):
        for ahead_col in range(SIDE):
            if ahead_row or ahead_col:
                pl.semaphore_signal(
                    barrier,
                    inc=1,
                    device_id=(
                        part,
                        lax.rem(row + ahead_row, SIDE),
                        lax.rem(col + ahead_col, SIDE),
                    ),
                    device_id_type=pl.DeviceIdType.MESH,
                )

    row_label = column_of(label_rows_ref, row)
    for c in range(SIDE):
        differ = jnp.bitwise_xor(row_label, label_rows_ref[c : c + 1, :])
        for m in range(8):
            mask[c, m] = jnp.where(differ == m, 1.0, 0.0).astype(mask.dtype)
    for m in range(8):
        one_hot[m] = jnp.where(row_label == m, 1.0, 0.0)
    total[...] = jnp.zeros_like(total)

    def fold(k, carry):
        shift = jnp.bitwise_xor(occ_ref[first_k + k], occ_ref[batch_size])
        screened = jnp.zeros((LANES, LANES), jnp.float32)
        for m in range(8):
            screened += screen_ref[first_k + k, m].astype(jnp.float32) * one_hot[m]
        screened = screened.astype(raw.dtype)
        for h in range(SIDE // 2):
            low = raw[k, :, h * LANES : (h + 1) * LANES] * mask[h, shift]
            g = h + SIDE // 2
            high = raw[k, :, g * LANES : (g + 1) * LANES] * mask[g, shift]
            shards[row, k, :, h * LANES : (h + 1) * LANES] = (low + high) * screened
        return carry

    def hop(distance, j, up):
        way = 0 if up else 1
        owner = row - distance if up else row + distance
        piece = shards.at[owner, span_of(j)]
        return remote(
            piece,
            piece,
            send_sem.at[way, distance, j],
            recv_sem.at[way, distance, j],
            row + 1 if up else row - 1,
            col,
        )

    def arrival(distance, j, up):
        way = 0 if up else 1
        owner = row - distance if up else row + distance
        piece = shards.at[owner, span_of(j)]
        return remote(
            piece,
            piece,
            send_sem.at[way, distance - 1, j],
            recv_sem.at[way, distance - 1, j],
            row - 1 if up else row + 1,
            col,
        )

    def accumulate(owner, j):
        def one(k, carry):
            rows = []
            for i in range(batch_size):
                shift = jnp.bitwise_xor(occ_ref[i], occ_ref[first_k + k])
                rows.append(amp[owner, i, k] * mask[owner, shift])
            total[...] += jnp.dot(
                jnp.concatenate(rows, axis=0),
                shards[owner, k],
                preferred_element_type=jnp.float32,
            )
            return carry

        lax.fori_loop(starts[j], starts[j + 1], one, 0)

    def give(j):
        span = span_of(j)
        return remote(
            amp_out.at[span], amp_in.at[span], give_send.at[j], give_recv.at[j], inner_row, col
        )

    def give_away():
        def one(k, carry):
            for i in range(batch_size):
                shift = jnp.bitwise_xor(occ_ref[i], occ_ref[first_k + k])
                for h in range(SIDE // 2):
                    g = h + SIDE // 2
                    amp_out[k, i, :, h * LANES : (h + 1) * LANES] = (
                        amp[h, i, k] * mask[h, shift] + amp[g, i, k] * mask[g, shift]
                    )
            return carry

        lax.fori_loop(0, starts[len(GIVEN)], one, 0)

    def accumulate_given(j):
        def one(k, carry):
            for c in range(SIDE):
                h = c % (SIDE // 2)
                rows = []
                for i in range(batch_size):
                    shift = jnp.bitwise_xor(occ_ref[i], occ_ref[first_k + k])
                    rows.append(
                        amp_in[k, i, :, h * LANES : (h + 1) * LANES] * end_mask[c, shift]
                    )
                end_total[...] += jnp.dot(
                    jnp.concatenate(rows, axis=0),
                    shards[c, k],
                    preferred_element_type=jnp.float32,
                )
            return carry

        lax.fori_loop(starts[j], starts[j + 1], one, 0)

    def sends(distance, j, up):
        if up:
            there = (row >= distance) & (row < SIDE - 1)
            return there if j >= len(GIVEN) else there & (row < SIDE - 2)
        there = (row + distance < SIDE) & (row > 0)
        return there if j >= len(GIVEN) else there & (row > 1)

    def gets(distance, j, up):
        if up:
            there = row >= distance
            return there if j >= len(GIVEN) else there & (row < SIDE - 1)
        there = row + distance < SIDE
        return there if j >= len(GIVEN) else there & (row > 0)

    for j in range(PIECES):
        raw_copies[j].wait()
        lax.fori_loop(starts[j], starts[j + 1], fold, 0)
        if j == 0:
            pl.semaphore_wait(barrier, SIDE * SIDE - 1)
        for up in (True, False):

            @pl.when(sends(0, j, up))
            def _():
                hop(0, j, up).start()

    for copy in amp_copies:
        copy.wait()

    @pl.when(is_end)
    def _():
        give_away()

    @pl.when(is_inner)
    def _():
        end_label = column_of(label_rows_ref, end_row)
        for c in range(SIDE):
            differ = jnp.bitwise_xor(end_label, label_rows_ref[c : c + 1, :])
            for m in range(8):
                end_mask[c, m] = jnp.where(differ == m, 1.0, 0.0).astype(end_mask.dtype)
        end_total[...] = jnp.zeros_like(end_total)
        for j in range(len(GIVEN)):
            accumulate(row, j)

    for j in range(len(GIVEN), PIECES):
        accumulate(row, j)

    for distance in range(1, SIDE):
        for j in range(PIECES):
            for up in (True, False):

                @pl.when(gets(distance, j, up))
                def _():
                    arrival(distance, j, up).wait_recv()

                if distance < SIDE - 1:

                    @pl.when(sends(distance, j, up))
                    def _():
                        hop(distance, j, up).start()

            for up in (True, False):

                @pl.when(gets(distance, j, up))
                def _():
                    accumulate(row - distance if up else row + distance, j)

        if distance == 1:

            @pl.when(is_end)
            def _():
                for j in range(len(GIVEN)):
                    give(j).start()

    share = total.shape[0] // SIDE

    def own_rows(ref, to_col):
        return ref.at[pl.ds(pl.multiple_of(to_col * share, share), share)]

    col_copies = []
    for ahead in range(1, SIDE):
        to_col = lax.rem(col + ahead, SIDE)
        copy = remote(
            own_rows(total, to_col),
            from_cols.at[ahead - 1],
            col_send.at[ahead - 1],
            col_recv.at[ahead - 1],
            row,
            to_col,
        )
        copy.start()
        col_copies.append(copy)

    def end_col_copy(ahead):
        to_col = lax.rem(col + ahead, SIDE)
        return remote(
            own_rows(end_total, to_col),
            end_cols.at[ahead - 1],
            give_col_send.at[ahead - 1],
            give_col_recv.at[ahead - 1],
            row,
            to_col,
        )

    def give_back():
        return remote(end_sum, from_inner, back_send, back_recv, end_row, col)

    @pl.when(is_inner)
    def _():
        for j in range(len(GIVEN)):
            give(j).wait_recv()
            accumulate_given(j)
        for ahead in range(1, SIDE):
            end_col_copy(ahead).start()
        summed = end_total[pl.ds(pl.multiple_of(col * share, share), share), :]
        for ahead in range(1, SIDE):
            end_col_copy(ahead).wait_recv()
            summed += end_cols[ahead - 1]
        end_sum[...] = summed
        give_back().start()
        from_inner[...] = jnp.zeros_like(from_inner)

    summed = total[pl.ds(pl.multiple_of(col * share, share), share), :]
    for ahead in range(1, SIDE):
        col_copies[ahead - 1].wait_recv()
        summed += from_cols[ahead - 1]

    @pl.when(is_end)
    def _():
        give_back().wait_recv()

    summed += from_inner[...]
    halves[0] = summed[:, :LANES]
    halves[1] = summed[:, LANES:]

    def deliver(ahead):
        to_row = lax.rem(row + ahead, SIDE)
        return remote(
            halves.at[lax.rem(to_row, 2)],
            landed.at[col],
            end_send.at[ahead],
            end_recv.at[col],
            to_row,
            row,
        )

    for ahead in range(1, SIDE):
        deliver(ahead).start()

    @pl.when(row != col)
    def _():
        deliver(0).start()

    @pl.when(row == col)
    def _():
        landed[col] = halves[lax.rem(row, 2)]

    def delivered(i):
        return remote(
            halves.at[0],
            landed.at[i],
            end_send.at[0],
            end_recv.at[i],
            lax.rem(row + 1, SIDE),
            col,
        )

    energy_of_a = energy_rows_ref[pl.ds(col, 1), :]
    energy_of_b = column_of(energy_rows_ref, row)
    wanted = jnp.bitwise_xor(
        jnp.bitwise_xor(row_label, label_rows_ref[pl.ds(col, 1), :]), occ_ref[batch_size]
    )
    for i in range(SIDE):

        @pl.when((row != col) | (col != i))
        def _():
            delivered(i).wait_recv()

        value = jnp.where(wanted == occ_ref[i], landed[i].T, 0.0)
        out_ref[:, i, :] = value / (
            occ_energy_ref[i] + occ_energy_ref[batch_size] - energy_of_a - energy_of_b
        )

    for ahead in range(1, SIDE):
        col_copies[ahead - 1].wait_send()
        deliver(ahead).wait_send()

    @pl.when(row != col)
    def _():
        deliver(0).wait_send()

    for distance in range(SIDE - 1):
        for j in range(PIECES):
            for up in (True, False):

                @pl.when(sends(distance, j, up))
                def _():
                    hop(distance, j, up).wait_send()

    @pl.when(is_end)
    def _():
        for j in range(len(GIVEN)):
            give(j).wait_send()

    @pl.when(is_inner)
    def _():
        for ahead in range(1, SIDE):
            end_col_copy(ahead).wait_send()
        give_back().wait_send()


def cycle_blocks(
    amplitudes, integrals, occ_irrep, vir_irrep, screen, occ_energy, vir_energy
):
    batch_size, occ_share, vir_share, vir_total = amplitudes.shape
    half = vir_total // 2
    bf16, f32 = jnp.bfloat16, jnp.float32
    given = sum(GIVEN)
    sizes = GIVEN + ((occ_share - given) // OWN,) * OWN
    vmem, smem, dma = pltpu.VMEM, pltpu.SMEM, pltpu.SemaphoreType.DMA
    hops = (2, SIDE - 1, PIECES)
    in_vmem = pl.BlockSpec(memory_space=vmem)
    in_smem = pl.BlockSpec(memory_space=smem)
    anywhere = pl.BlockSpec(memory_space=pl.ANY)
    return pl.pallas_call(
        functools.partial(cycle_kernel, sizes),
        out_shape=jax.ShapeDtypeStruct((LANES, batch_size, LANES), f32),
        in_specs=[in_smem, in_smem, in_smem, in_vmem, in_vmem, anywhere, anywhere],
        out_specs=in_vmem,
        scratch_shapes=[
            vmem((occ_share, vir_share, vir_total), bf16),
            vmem((SIDE, batch_size, occ_share, vir_share, LANES), bf16),
            vmem((SIDE, 8, vir_share, LANES), bf16),
            vmem((8, vir_share, LANES), f32),
            vmem((SIDE, occ_share, vir_share, half), bf16),
            vmem((batch_size * vir_share, half), f32),
            vmem((SIDE - 1, vir_share, half), f32),
            vmem((2, vir_share, LANES), f32),
            vmem((SIDE, vir_share, LANES), f32),
            vmem((SIDE, 8, vir_share, LANES), bf16),
            vmem((given, batch_size, vir_share, half), bf16),
            vmem((given, batch_size, vir_share, half), bf16),
            vmem((batch_size * vir_share, half), f32),
            vmem((SIDE - 1, vir_share, half), f32),
            vmem((vir_share, half), f32),
            vmem((vir_share, half), f32),
            dma((PIECES,)),
            dma((SIDE,)),
            dma(hops),
            dma(hops),
            dma((SIDE - 1,)),
            dma((SIDE - 1,)),
            dma((SIDE,)),
            dma((SIDE,)),
            dma((len(GIVEN),)),
            dma((len(GIVEN),)),
            dma((SIDE - 1,)),
            dma((SIDE - 1,)),
            dma,
            dma,
        ],
        compiler_params=pltpu.CompilerParams(
            collective_id=0, has_side_effects=True, vmem_limit_bytes=52 * 1024 * 1024
        ),
        name="cycle_blocks",
    )(
        occ_irrep,
        screen,
        occ_energy,
        vir_irrep.reshape(SIDE, LANES),
        vir_energy.reshape(SIDE, LANES),
        integrals,
        amplitudes,
    )


def fits_kernel(row_count, column_count, amplitudes):
    batch_size, occ_share, vir_share, vir_total = amplitudes.shape
    return (
        row_count == column_count == batch_size == SIDE
        and vir_share == LANES
        and vir_total == SIDE * LANES
        and occ_share > sum(GIVEN)
        and (occ_share - sum(GIVEN)) % OWN == 0
    )


def on_device(amplitudes, integrals, occ_irrep, vir_irrep, screen, occ_energy, vir_energy):
    row_count = lax.axis_size("row")
    column_count = lax.axis_size("col")
    row, col = lax.axis_index("row"), lax.axis_index("col")
    batch_size, occ_share, vir_share, vir_total = amplitudes.shape
    if fits_kernel(row_count, column_count, amplitudes):
        return cycle_blocks(
            amplitudes, integrals, occ_irrep, vir_irrep, screen, occ_energy, vir_energy
        )
    half = vir_total // 2
    vir_columns = vir_total // column_count
    occ_offset = col * occ_share
    occ_local = lax.dynamic_slice_in_dim(occ_irrep, occ_offset, occ_share)
    vir_local = lax.dynamic_slice_in_dim(vir_irrep, row * vir_share, vir_share)
    screen_rows = lax.dynamic_slice_in_dim(screen, occ_offset, occ_share, 0)
    pair_label = occ_irrep[batch_size]

    folded = folded_integrals(
        integrals, occ_local, vir_local, vir_irrep, screen_rows, pair_label
    )
    gathered = lax.all_gather(folded, "row", axis=1, tiled=True)
    shift = jnp.bitwise_xor(occ_irrep[:batch_size, None], occ_local[None, :])
    keep_amp = (
        jnp.bitwise_xor(shift[:, :, None], vir_local[None, None, :])[:, :, :, None]
        == vir_irrep[None, None, None, :]
    )
    amp_kept = jnp.where(keep_amp, amplitudes, jnp.zeros_like(amplitudes))
    partial = lax.dot_general(
        amp_kept, gathered, (((1, 3), (0, 1)), ((), ())), preferred_element_type=jnp.float32
    )
    whole = lax.all_gather(lax.psum(partial, "col"), "row", axis=1, tiled=True)
    cycle = lax.dynamic_slice_in_dim(whole, col * vir_columns, vir_columns, 1)
    cycle = lax.dynamic_slice_in_dim(cycle, (row * vir_share) % half, vir_share, 2)
    cycle = jnp.transpose(cycle, (2, 0, 1))
    col_irrep = lax.dynamic_slice_in_dim(vir_irrep, col * vir_columns, vir_columns)
    kept = (
        jnp.bitwise_xor(occ_irrep[:batch_size, None], pair_label ^ col_irrep[None, :])[None]
        == vir_local[:, None, None]
    )
    cycle = jnp.where(kept, cycle, 0.0)
    energy_cols = lax.dynamic_slice_in_dim(vir_energy, col * vir_columns, vir_columns)
    energy_rows = lax.dynamic_slice_in_dim(vir_energy, row * vir_share, vir_share)
    denominator = (
        occ_energy[:batch_size][None, :, None]
        + occ_energy[batch_size]
        - energy_cols[None, None, :]
        - energy_rows[:, None, None]
    )
    return cycle / denominator


def solution(mesh):
    in_specs = (
        P("parts", "col", "row", None),
        P(("parts", "col"), "row", None),
        P("parts"),
        P("parts"),
        P("parts", None),
        P("parts"),
        P("parts"),
    )
    out_specs = P("row", "parts", "col")
    return jax.shard_map(
        on_device, mesh=mesh, in_specs=in_specs, out_specs=out_specs, check_vma=False
    )
```

```python
import functools

import jax
import jax.numpy as jnp
from jax import lax
from jax.experimental import pallas as pl
from jax.experimental.pallas import tpu as pltpu
from jax.sharding import PartitionSpec as P

LANES = 128
SIDE = 4
GIVEN = (4, 3)
OWN = 3
PIECES = OWN + len(GIVEN)


def folded_integrals(integrals, occ_local, vir_local, vir_irrep, screen_rows, pair_label):
    half = vir_irrep.shape[0] // 2
    irrep_codes = jnp.arange(8, dtype=jnp.int32)
    screen_local = jnp.sum(
        screen_rows[:, None, :] * (vir_local[None, :, None] == irrep_codes).astype(jnp.int32),
        axis=2,
    )
    wanted = jnp.bitwise_xor(jnp.bitwise_xor(occ_local[:, None], vir_local[None, :]), pair_label)
    wanted = jnp.where(screen_local == 1, wanted, -1)[:, :, None]
    zeros = jnp.zeros((), integrals.dtype)
    low = jnp.where(wanted == vir_irrep[None, None, :half], integrals[:, :, :half], zeros)
    return jnp.where(wanted == vir_irrep[None, None, half:], integrals[:, :, half:], low)


def cycle_kernel(
    sizes,
    occ_ref,
    screen_ref,
    occ_energy_ref,
    label_rows_ref,
    energy_rows_ref,
    int_hbm,
    amp_hbm,
    out_ref,
    raw,
    amp,
    mask,
    one_hot,
    shards,
    total,
    from_cols,
    halves,
    landed,
    end_mask,
    amp_out,
    amp_in,
    end_total,
    end_cols,
    end_sum,
    from_inner,
    raw_sem,
    amp_sem,
    send_sem,
    recv_sem,
    col_send,
    col_recv,
    end_send,
    end_recv,
    give_send,
    give_recv,
    give_col_send,
    give_col_recv,
    back_send,
    back_recv,
):
    part, row, col = lax.axis_index("parts"), lax.axis_index("row"), lax.axis_index("col")
    batch_size = amp.shape[1]
    occ_share = raw.shape[0]
    first_k = col * occ_share
    is_end = (row == 0) | (row == SIDE - 1)
    is_inner = (row > 0) & (row < SIDE - 1)
    upper = row // (SIDE // 2)
    end_row = upper * (SIDE - 1)
    inner_row = 1 + upper * (SIDE - 3)
    starts = [sum(sizes[:j]) for j in range(PIECES + 1)]

    def span_of(j):
        return pl.ds(starts[j], sizes[j])

    def column_of(ref, which):
        return jnp.broadcast_to(ref[pl.ds(which, 1), :], (LANES, LANES)).T

    def remote(source, target, send, recv, to_row, to_col):
        return pltpu.make_async_remote_copy(
            src_ref=source,
            dst_ref=target,
            send_sem=send,
            recv_sem=recv,
            device_id=(part, to_row, to_col),
            device_id_type=pl.DeviceIdType.MESH,
        )

    raw_copies = []
    for j in range(PIECES):
        span = span_of(j)
        copy = pltpu.make_async_copy(int_hbm.at[span], raw.at[span], raw_sem.at[j])
        copy.start()
        raw_copies.append(copy)
    amp_copies = []
    for c in range(SIDE):
        copy = pltpu.make_async_copy(
            amp_hbm.at[:, :, :, pl.ds(c * LANES, LANES)], amp.at[c], amp_sem.at[c]
        )
        copy.start()
        amp_copies.append(copy)

    barrier = pltpu.get_barrier_semaphore()
    for ahead_row in range(SIDE):
        for ahead_col in range(SIDE):
            if ahead_row or ahead_col:
                pl.semaphore_signal(
                    barrier,
                    inc=1,
                    device_id=(
                        part,
                        lax.rem(row + ahead_row, SIDE),
                        lax.rem(col + ahead_col, SIDE),
                    ),
                    device_id_type=pl.DeviceIdType.MESH,
                )

    row_label = column_of(label_rows_ref, row)
    for c in range(SIDE):
        differ = jnp.bitwise_xor(row_label, label_rows_ref[c : c + 1, :])
        for m in range(8):
            mask[c, m] = jnp.where(differ == m, 1.0, 0.0).astype(mask.dtype)
    for m in range(8):
        one_hot[m] = jnp.where(row_label == m, 1.0, 0.0)
    total[...] = jnp.zeros_like(total)

    def fold(k, carry):
        shift = jnp.bitwise_xor(occ_ref[first_k + k], occ_ref[batch_size])
        screened = jnp.zeros((LANES, LANES), jnp.float32)
        for m in range(8):
            screened += screen_ref[first_k + k, m].astype(jnp.float32) * one_hot[m]
        screened = screened.astype(raw.dtype)
        for h in range(SIDE // 2):
            low = raw[k, :, h * LANES : (h + 1) * LANES] * mask[h, shift]
            g = h + SIDE // 2
            high = raw[k, :, g * LANES : (g + 1) * LANES] * mask[g, shift]
            shards[row, k, :, h * LANES : (h + 1) * LANES] = (low + high) * screened
        return carry

    def hop(distance, j, up):
        way = 0 if up else 1
        owner = row - distance if up else row + distance
        piece = shards.at[owner, span_of(j)]
        return remote(
            piece,
            piece,
            send_sem.at[way, distance, j],
            recv_sem.at[way, distance, j],
            row + 1 if up else row - 1,
            col,
        )

    def arrival(distance, j, up):
        way = 0 if up else 1
        owner = row - distance if up else row + distance
        piece = shards.at[owner, span_of(j)]
        return remote(
            piece,
            piece,
            send_sem.at[way, distance - 1, j],
            recv_sem.at[way, distance - 1, j],
            row - 1 if up else row + 1,
            col,
        )

    def accumulate(owner, j):
        def one(k, carry):
            rows = []
            for i in range(batch_size):
                shift = jnp.bitwise_xor(occ_ref[i], occ_ref[first_k + k])
                rows.append(amp[owner, i, k] * mask[owner, shift])
            total[...] += jnp.dot(
                jnp.concatenate(rows, axis=0),
                shards[owner, k],
                preferred_element_type=jnp.float32,
            )
            return carry

        lax.fori_loop(starts[j], starts[j + 1], one, 0)

    def give(j):
        span = pl.ds(starts[j] - starts[OWN], sizes[j])
        return remote(
            amp_out.at[span],
            amp_in.at[span],
            give_send.at[j - OWN],
            give_recv.at[j - OWN],
            inner_row,
            col,
        )

    def give_away():
        def one(k, carry):
            for i in range(batch_size):
                shift = jnp.bitwise_xor(occ_ref[i], occ_ref[first_k + k])
                for h in range(SIDE // 2):
                    g = h + SIDE // 2
                    amp_out[k - starts[OWN], i, :, h * LANES : (h + 1) * LANES] = (
                        amp[h, i, k] * mask[h, shift] + amp[g, i, k] * mask[g, shift]
                    )
            return carry

        lax.fori_loop(starts[OWN], starts[PIECES], one, 0)

    def accumulate_given(j):
        def one(k, carry):
            for c in range(SIDE):
                h = c % (SIDE // 2)
                rows = []
                for i in range(batch_size):
                    shift = jnp.bitwise_xor(occ_ref[i], occ_ref[first_k + k])
                    rows.append(
                        amp_in[k - starts[OWN], i, :, h * LANES : (h + 1) * LANES]
                        * end_mask[c, shift]
                    )
                end_total[...] += jnp.dot(
                    jnp.concatenate(rows, axis=0),
                    shards[c, k],
                    preferred_element_type=jnp.float32,
                )
            return carry

        lax.fori_loop(starts[j], starts[j + 1], one, 0)

    def sends(distance, j, up):
        if up:
            there = (row >= distance) & (row < SIDE - 1)
            return there if j < OWN else there & (row < SIDE - 2)
        there = (row + distance < SIDE) & (row > 0)
        return there if j < OWN else there & (row > 1)

    def gets(distance, j, up):
        if up:
            there = row >= distance
            return there if j < OWN else there & (row < SIDE - 1)
        there = row + distance < SIDE
        return there if j < OWN else there & (row > 0)

    for j in range(PIECES):
        raw_copies[j].wait()
        lax.fori_loop(starts[j], starts[j + 1], fold, 0)
        if j == 0:
            pl.semaphore_wait(barrier, SIDE * SIDE - 1)
        for up in (True, False):

            @pl.when(sends(0, j, up))
            def _():
                hop(0, j, up).start()

    for copy in amp_copies:
        copy.wait()

    @pl.when(is_end)
    def _():
        give_away()

    @pl.when(is_inner)
    def _():
        end_label = column_of(label_rows_ref, end_row)
        for c in range(SIDE):
            differ = jnp.bitwise_xor(end_label, label_rows_ref[c : c + 1, :])
            for m in range(8):
                end_mask[c, m] = jnp.where(differ == m, 1.0, 0.0).astype(end_mask.dtype)
        end_total[...] = jnp.zeros_like(end_total)
        for j in range(OWN, PIECES):
            accumulate(row, j)

    for j in range(OWN):
        accumulate(row, j)

    for distance in range(1, SIDE):
        for j in range(PIECES):
            for up in (True, False):

                @pl.when(gets(distance, j, up))
                def _():
                    arrival(distance, j, up).wait_recv()

                if distance < SIDE - 1:

                    @pl.when(sends(distance, j, up))
                    def _():
                        hop(distance, j, up).start()

            for up in (True, False):

                @pl.when(gets(distance, j, up))
                def _():
                    accumulate(row - distance if up else row + distance, j)

        if distance == 1:

            @pl.when(is_end)
            def _():
                for j in range(OWN, PIECES):
                    give(j).start()

    share = total.shape[0] // SIDE

    def own_rows(to_col):
        return pl.ds(pl.multiple_of(to_col * share, share), share)

    def col_copy(source, target, send, recv, h, ahead):
        to_col = lax.rem(col + ahead, SIDE)
        return remote(
            source.at[own_rows(to_col), pl.ds(h * LANES, LANES)],
            target.at[ahead - 1, h],
            send.at[h, ahead - 1],
            recv.at[h, ahead - 1],
            row,
            to_col,
        )

    own_copy = functools.partial(col_copy, total, from_cols, col_send, col_recv)
    end_copy = functools.partial(col_copy, end_total, end_cols, give_col_send, give_col_recv)

    def give_back(h):
        return remote(
            end_sum.at[h], from_inner.at[h], back_send.at[h], back_recv.at[h], end_row, col
        )

    for h in range(2):
        for ahead in range(1, SIDE):
            own_copy(h, ahead).start()

    @pl.when(is_inner)
    def _():
        for j in range(OWN, PIECES):
            give(j).wait_recv()
            accumulate_given(j)
        for h in range(2):
            for ahead in range(1, SIDE):
                end_copy(h, ahead).start()
        for h in range(2):
            summed = end_total[own_rows(col), h * LANES : (h + 1) * LANES]
            for ahead in range(1, SIDE):
                end_copy(h, ahead).wait_recv()
                summed += end_cols[ahead - 1, h]
            end_sum[h] = summed
            give_back(h).start()
        from_inner[...] = jnp.zeros_like(from_inner)

    def deliver(to_row):
        return remote(
            halves.at[to_row % 2],
            landed.at[col],
            end_send.at[to_row],
            end_recv.at[col],
            to_row,
            row,
        )

    for h in range(2):
        summed = total[own_rows(col), h * LANES : (h + 1) * LANES]
        for ahead in range(1, SIDE):
            own_copy(h, ahead).wait_recv()
            summed += from_cols[ahead - 1, h]

        @pl.when(is_end)
        def _():
            give_back(h).wait_recv()

        halves[h] = summed + from_inner[h]
        for to_row in (h, h + 2):

            @pl.when((row != to_row) | (col != to_row))
            def _():
                deliver(to_row).start()

            @pl.when((row == to_row) & (col == to_row))
            def _():
                landed[to_row] = halves[h]

    def delivered(i):
        return remote(
            halves.at[0],
            landed.at[i],
            end_send.at[0],
            end_recv.at[i],
            lax.rem(row + 1, SIDE),
            col,
        )

    energy_of_a = energy_rows_ref[pl.ds(col, 1), :]
    energy_of_b = column_of(energy_rows_ref, row)
    wanted = jnp.bitwise_xor(
        jnp.bitwise_xor(row_label, label_rows_ref[pl.ds(col, 1), :]), occ_ref[batch_size]
    )
    for i in range(SIDE):

        @pl.when((row != col) | (col != i))
        def _():
            delivered(i).wait_recv()

        value = jnp.where(wanted == occ_ref[i], landed[i].T, 0.0)
        out_ref[:, i, :] = value / (
            occ_energy_ref[i] + occ_energy_ref[batch_size] - energy_of_a - energy_of_b
        )

    for h in range(2):
        for ahead in range(1, SIDE):
            own_copy(h, ahead).wait_send()
    for to_row in range(SIDE):

        @pl.when((row != to_row) | (col != to_row))
        def _():
            deliver(to_row).wait_send()

    for distance in range(SIDE - 1):
        for j in range(PIECES):
            for up in (True, False):

                @pl.when(sends(distance, j, up))
                def _():
                    hop(distance, j, up).wait_send()

    @pl.when(is_end)
    def _():
        for j in range(OWN, PIECES):
            give(j).wait_send()

    @pl.when(is_inner)
    def _():
        for h in range(2):
            for ahead in range(1, SIDE):
                end_copy(h, ahead).wait_send()
            give_back(h).wait_send()


def cycle_blocks(
    amplitudes, integrals, occ_irrep, vir_irrep, screen, occ_energy, vir_energy
):
    batch_size, occ_share, vir_share, vir_total = amplitudes.shape
    half = vir_total // 2
    bf16, f32 = jnp.bfloat16, jnp.float32
    given = sum(GIVEN)
    sizes = ((occ_share - given) // OWN,) * OWN + GIVEN
    vmem, smem, dma = pltpu.VMEM, pltpu.SMEM, pltpu.SemaphoreType.DMA
    hops = (2, SIDE - 1, PIECES)
    in_vmem = pl.BlockSpec(memory_space=vmem)
    in_smem = pl.BlockSpec(memory_space=smem)
    anywhere = pl.BlockSpec(memory_space=pl.ANY)
    return pl.pallas_call(
        functools.partial(cycle_kernel, sizes),
        out_shape=jax.ShapeDtypeStruct((LANES, batch_size, LANES), f32),
        in_specs=[in_smem, in_smem, in_smem, in_vmem, in_vmem, anywhere, anywhere],
        out_specs=in_vmem,
        scratch_shapes=[
            vmem((occ_share, vir_share, vir_total), bf16),
            vmem((SIDE, batch_size, occ_share, vir_share, LANES), bf16),
            vmem((SIDE, 8, vir_share, LANES), bf16),
            vmem((8, vir_share, LANES), f32),
            vmem((SIDE, occ_share, vir_share, half), bf16),
            vmem((batch_size * vir_share, half), f32),
            vmem((SIDE - 1, 2, vir_share, LANES), f32),
            vmem((2, vir_share, LANES), f32),
            vmem((SIDE, vir_share, LANES), f32),
            vmem((SIDE, 8, vir_share, LANES), bf16),
            vmem((given, batch_size, vir_share, half), bf16),
            vmem((given, batch_size, vir_share, half), bf16),
            vmem((batch_size * vir_share, half), f32),
            vmem((SIDE - 1, 2, vir_share, LANES), f32),
            vmem((2, vir_share, LANES), f32),
            vmem((2, vir_share, LANES), f32),
            dma((PIECES,)),
            dma((SIDE,)),
            dma(hops),
            dma(hops),
            dma((2, SIDE - 1)),
            dma((2, SIDE - 1)),
            dma((SIDE,)),
            dma((SIDE,)),
            dma((len(GIVEN),)),
            dma((len(GIVEN),)),
            dma((2, SIDE - 1)),
            dma((2, SIDE - 1)),
            dma((2,)),
            dma((2,)),
        ],
        compiler_params=pltpu.CompilerParams(
            collective_id=0, has_side_effects=True, vmem_limit_bytes=52 * 1024 * 1024
        ),
        name="cycle_blocks",
    )(
        occ_irrep,
        screen,
        occ_energy,
        vir_irrep.reshape(SIDE, LANES),
        vir_energy.reshape(SIDE, LANES),
        integrals,
        amplitudes,
    )


def fits_kernel(row_count, column_count, amplitudes):
    batch_size, occ_share, vir_share, vir_total = amplitudes.shape
    return (
        row_count == column_count == batch_size == SIDE
        and vir_share == LANES
        and vir_total == SIDE * LANES
        and occ_share > sum(GIVEN)
        and (occ_share - sum(GIVEN)) % OWN == 0
    )


def on_device(amplitudes, integrals, occ_irrep, vir_irrep, screen, occ_energy, vir_energy):
    row_count = lax.axis_size("row")
    column_count = lax.axis_size("col")
    row, col = lax.axis_index("row"), lax.axis_index("col")
    batch_size, occ_share, vir_share, vir_total = amplitudes.shape
    if fits_kernel(row_count, column_count, amplitudes):
        return cycle_blocks(
            amplitudes, integrals, occ_irrep, vir_irrep, screen, occ_energy, vir_energy
        )
    half = vir_total // 2
    vir_columns = vir_total // column_count
    occ_offset = col * occ_share
    occ_local = lax.dynamic_slice_in_dim(occ_irrep, occ_offset, occ_share)
    vir_local = lax.dynamic_slice_in_dim(vir_irrep, row * vir_share, vir_share)
    screen_rows = lax.dynamic_slice_in_dim(screen, occ_offset, occ_share, 0)
    pair_label = occ_irrep[batch_size]

    folded = folded_integrals(
        integrals, occ_local, vir_local, vir_irrep, screen_rows, pair_label
    )
    gathered = lax.all_gather(folded, "row", axis=1, tiled=True)
    shift = jnp.bitwise_xor(occ_irrep[:batch_size, None], occ_local[None, :])
    keep_amp = (
        jnp.bitwise_xor(shift[:, :, None], vir_local[None, None, :])[:, :, :, None]
        == vir_irrep[None, None, None, :]
    )
    amp_kept = jnp.where(keep_amp, amplitudes, jnp.zeros_like(amplitudes))
    partial = lax.dot_general(
        amp_kept, gathered, (((1, 3), (0, 1)), ((), ())), preferred_element_type=jnp.float32
    )
    whole = lax.all_gather(lax.psum(partial, "col"), "row", axis=1, tiled=True)
    cycle = lax.dynamic_slice_in_dim(whole, col * vir_columns, vir_columns, 1)
    cycle = lax.dynamic_slice_in_dim(cycle, (row * vir_share) % half, vir_share, 2)
    cycle = jnp.transpose(cycle, (2, 0, 1))
    col_irrep = lax.dynamic_slice_in_dim(vir_irrep, col * vir_columns, vir_columns)
    kept = (
        jnp.bitwise_xor(occ_irrep[:batch_size, None], pair_label ^ col_irrep[None, :])[None]
        == vir_local[:, None, None]
    )
    cycle = jnp.where(kept, cycle, 0.0)
    energy_cols = lax.dynamic_slice_in_dim(vir_energy, col * vir_columns, vir_columns)
    energy_rows = lax.dynamic_slice_in_dim(vir_energy, row * vir_share, vir_share)
    denominator = (
        occ_energy[:batch_size][None, :, None]
        + occ_energy[batch_size]
        - energy_cols[None, None, :]
        - energy_rows[:, None, None]
    )
    return cycle / denominator


def solution(mesh):
    in_specs = (
        P("parts", "col", "row", None),
        P(("parts", "col"), "row", None),
        P("parts"),
        P("parts"),
        P("parts", None),
        P("parts"),
        P("parts"),
    )
    out_specs = P("row", "parts", "col")
    return jax.shard_map(
        on_device, mesh=mesh, in_specs=in_specs, out_specs=out_specs, check_vma=False
    )
```

```python
import functools

import jax
import jax.numpy as jnp
from jax import lax
from jax.experimental import pallas as pl
from jax.experimental.pallas import tpu as pltpu
from jax.sharding import PartitionSpec as P

LANES = 128
SIDE = 4
GIVEN = (4, 3)
OWN = 3
PIECES = OWN + len(GIVEN)


def folded_integrals(integrals, occ_local, vir_local, vir_irrep, screen_rows, pair_label):
    half = vir_irrep.shape[0] // 2
    irrep_codes = jnp.arange(8, dtype=jnp.int32)
    screen_local = jnp.sum(
        screen_rows[:, None, :] * (vir_local[None, :, None] == irrep_codes).astype(jnp.int32),
        axis=2,
    )
    wanted = jnp.bitwise_xor(jnp.bitwise_xor(occ_local[:, None], vir_local[None, :]), pair_label)
    wanted = jnp.where(screen_local == 1, wanted, -1)[:, :, None]
    zeros = jnp.zeros((), integrals.dtype)
    low = jnp.where(wanted == vir_irrep[None, None, :half], integrals[:, :, :half], zeros)
    return jnp.where(wanted == vir_irrep[None, None, half:], integrals[:, :, half:], low)


def cycle_kernel(
    sizes,
    screen_ref,
    occ_hbm,
    occ_energy_hbm,
    label_rows_hbm,
    energy_rows_hbm,
    int_hbm,
    amp_hbm,
    out_ref,
    occ_ref,
    occ_energy_ref,
    label_rows_ref,
    energy_rows_ref,
    small_sem,
    raw,
    amp,
    mask,
    one_hot,
    shards,
    total,
    from_cols,
    halves,
    landed,
    end_mask,
    amp_out,
    amp_in,
    end_total,
    end_cols,
    end_sum,
    from_inner,
    raw_sem,
    amp_sem,
    send_sem,
    recv_sem,
    col_send,
    col_recv,
    end_send,
    end_recv,
    give_send,
    give_recv,
    give_col_send,
    give_col_recv,
    back_send,
    back_recv,
):
    part, row, col = lax.axis_index("parts"), lax.axis_index("row"), lax.axis_index("col")
    batch_size = amp.shape[1]
    occ_share = raw.shape[0]
    first_k = col * occ_share
    is_end = (row == 0) | (row == SIDE - 1)
    is_inner = (row > 0) & (row < SIDE - 1)
    upper = row // (SIDE // 2)
    end_row = upper * (SIDE - 1)
    inner_row = 1 + upper * (SIDE - 3)
    starts = [sum(sizes[:j]) for j in range(PIECES + 1)]

    def span_of(j):
        return pl.ds(starts[j], sizes[j])

    def column_of(ref, which):
        return jnp.broadcast_to(ref[pl.ds(which, 1), :], (LANES, LANES)).T

    def remote(source, target, send, recv, to_row, to_col):
        return pltpu.make_async_remote_copy(
            src_ref=source,
            dst_ref=target,
            send_sem=send,
            recv_sem=recv,
            device_id=(part, to_row, to_col),
            device_id_type=pl.DeviceIdType.MESH,
        )

    small_copies = []
    for n, (source, target) in enumerate(
        (
            (occ_hbm, occ_ref),
            (label_rows_hbm, label_rows_ref),
            (occ_energy_hbm, occ_energy_ref),
            (energy_rows_hbm, energy_rows_ref),
        )
    ):
        copy = pltpu.make_async_copy(source, target, small_sem.at[n])
        copy.start()
        small_copies.append(copy)
    raw_copies = []
    for j in range(PIECES):
        span = span_of(j)
        copy = pltpu.make_async_copy(int_hbm.at[span], raw.at[span], raw_sem.at[j])
        copy.start()
        raw_copies.append(copy)
    amp_copies = []
    for c in range(SIDE):
        copy = pltpu.make_async_copy(
            amp_hbm.at[:, :, :, pl.ds(c * LANES, LANES)], amp.at[c], amp_sem.at[c]
        )
        copy.start()
        amp_copies.append(copy)

    barrier = pltpu.get_barrier_semaphore()
    for ahead_row in range(SIDE):
        for ahead_col in range(SIDE):
            if ahead_row or ahead_col:
                pl.semaphore_signal(
                    barrier,
                    inc=1,
                    device_id=(
                        part,
                        lax.rem(row + ahead_row, SIDE),
                        lax.rem(col + ahead_col, SIDE),
                    ),
                    device_id_type=pl.DeviceIdType.MESH,
                )

    for copy in small_copies:
        copy.wait()
    row_label = column_of(label_rows_ref, row)
    for c in range(SIDE):
        differ = jnp.bitwise_xor(row_label, label_rows_ref[c : c + 1, :])
        for m in range(8):
            mask[c, m] = jnp.where(differ == m, 1.0, 0.0).astype(mask.dtype)
    for m in range(8):
        one_hot[m] = jnp.where(row_label == m, 1.0, 0.0)
    total[...] = jnp.zeros_like(total)

    def fold(k, carry):
        shift = jnp.bitwise_xor(occ_ref[first_k + k], occ_ref[batch_size])
        screened = jnp.zeros((LANES, LANES), jnp.float32)
        for m in range(8):
            screened += screen_ref[first_k + k, m].astype(jnp.float32) * one_hot[m]
        screened = screened.astype(raw.dtype)
        for h in range(SIDE // 2):
            low = raw[k, :, h * LANES : (h + 1) * LANES] * mask[h, shift]
            g = h + SIDE // 2
            high = raw[k, :, g * LANES : (g + 1) * LANES] * mask[g, shift]
            shards[row, k, :, h * LANES : (h + 1) * LANES] = (low + high) * screened
        return carry

    def hop(distance, j, up):
        way = 0 if up else 1
        owner = row - distance if up else row + distance
        piece = shards.at[owner, span_of(j)]
        return remote(
            piece,
            piece,
            send_sem.at[way, distance, j],
            recv_sem.at[way, distance, j],
            row + 1 if up else row - 1,
            col,
        )

    def arrival(distance, j, up):
        way = 0 if up else 1
        owner = row - distance if up else row + distance
        piece = shards.at[owner, span_of(j)]
        return remote(
            piece,
            piece,
            send_sem.at[way, distance - 1, j],
            recv_sem.at[way, distance - 1, j],
            row - 1 if up else row + 1,
            col,
        )

    def accumulate(owner, j):
        def one(k, carry):
            rows = []
            for i in range(batch_size):
                shift = jnp.bitwise_xor(occ_ref[i], occ_ref[first_k + k])
                rows.append(amp[owner, i, k] * mask[owner, shift])
            total[...] += jnp.dot(
                jnp.concatenate(rows, axis=0),
                shards[owner, k],
                preferred_element_type=jnp.float32,
            )
            return carry

        lax.fori_loop(starts[j], starts[j + 1], one, 0)

    def give(j):
        span = pl.ds(starts[j] - starts[OWN], sizes[j])
        return remote(
            amp_out.at[span],
            amp_in.at[span],
            give_send.at[j - OWN],
            give_recv.at[j - OWN],
            inner_row,
            col,
        )

    def give_away():
        def one(k, carry):
            for i in range(batch_size):
                shift = jnp.bitwise_xor(occ_ref[i], occ_ref[first_k + k])
                for h in range(SIDE // 2):
                    g = h + SIDE // 2
                    amp_out[k - starts[OWN], i, :, h * LANES : (h + 1) * LANES] = (
                        amp[h, i, k] * mask[h, shift] + amp[g, i, k] * mask[g, shift]
                    )
            return carry

        lax.fori_loop(starts[OWN], starts[PIECES], one, 0)

    def accumulate_given(j):
        def one(k, carry):
            rows = []
            for i in range(batch_size):
                shift = jnp.bitwise_xor(occ_ref[i], occ_ref[first_k + k])
                blocks = []
                for c in range(SIDE):
                    h = c % (SIDE // 2)
                    blocks.append(
                        amp_in[k - starts[OWN], i, :, h * LANES : (h + 1) * LANES]
                        * end_mask[c, shift]
                    )
                rows.append(jnp.concatenate(blocks, axis=1))
            end_total[...] += jnp.dot(
                jnp.concatenate(rows, axis=0),
                jnp.concatenate([shards[c, k] for c in range(SIDE)], axis=0),
                preferred_element_type=jnp.float32,
            )
            return carry

        lax.fori_loop(starts[j], starts[j + 1], one, 0)

    def sends(distance, j, up):
        if up:
            there = (row >= distance) & (row < SIDE - 1)
            return there if j < OWN else there & (row < SIDE - 2)
        there = (row + distance < SIDE) & (row > 0)
        return there if j < OWN else there & (row > 1)

    def gets(distance, j, up):
        if up:
            there = row >= distance
            return there if j < OWN else there & (row < SIDE - 1)
        there = row + distance < SIDE
        return there if j < OWN else there & (row > 0)

    for j in range(PIECES):
        raw_copies[j].wait()
        lax.fori_loop(starts[j], starts[j + 1], fold, 0)
        if j == 0:
            pl.semaphore_wait(barrier, SIDE * SIDE - 1)
        for up in (True, False):

            @pl.when(sends(0, j, up))
            def _():
                hop(0, j, up).start()

    for copy in amp_copies:
        copy.wait()

    @pl.when(is_end)
    def _():
        give_away()

    @pl.when(is_inner)
    def _():
        end_label = column_of(label_rows_ref, end_row)
        for c in range(SIDE):
            differ = jnp.bitwise_xor(end_label, label_rows_ref[c : c + 1, :])
            for m in range(8):
                end_mask[c, m] = jnp.where(differ == m, 1.0, 0.0).astype(end_mask.dtype)
        end_total[...] = jnp.zeros_like(end_total)
        for j in range(OWN, PIECES):
            accumulate(row, j)

    for j in range(OWN):
        accumulate(row, j)

    for distance in range(1, SIDE):
        for j in range(PIECES):
            for up in (True, False):

                @pl.when(gets(distance, j, up))
                def _():
                    arrival(distance, j, up).wait_recv()

                if distance < SIDE - 1:

                    @pl.when(sends(distance, j, up))
                    def _():
                        hop(distance, j, up).start()

            for up in (True, False):

                @pl.when(gets(distance, j, up))
                def _():
                    accumulate(row - distance if up else row + distance, j)

        if distance == 1:

            @pl.when(is_end)
            def _():
                for j in range(OWN, PIECES):
                    give(j).start()

    share = total.shape[0] // SIDE

    def own_rows(to_col):
        return pl.ds(pl.multiple_of(to_col * share, share), share)

    def col_copy(source, target, send, recv, h, ahead):
        to_col = lax.rem(col + ahead, SIDE)
        return remote(
            source.at[own_rows(to_col), pl.ds(h * LANES, LANES)],
            target.at[ahead - 1, h],
            send.at[h, ahead - 1],
            recv.at[h, ahead - 1],
            row,
            to_col,
        )

    own_copy = functools.partial(col_copy, total, from_cols, col_send, col_recv)
    end_copy = functools.partial(col_copy, end_total, end_cols, give_col_send, give_col_recv)

    def give_back(h):
        return remote(
            end_sum.at[h], from_inner.at[h], back_send.at[h], back_recv.at[h], end_row, col
        )

    for h in range(2):
        for ahead in range(1, SIDE):
            own_copy(h, ahead).start()

    @pl.when(is_inner)
    def _():
        for j in range(OWN, PIECES):
            give(j).wait_recv()
            accumulate_given(j)
        for h in range(2):
            for ahead in range(1, SIDE):
                end_copy(h, ahead).start()
        for h in range(2):
            summed = end_total[own_rows(col), h * LANES : (h + 1) * LANES]
            for ahead in range(1, SIDE):
                end_copy(h, ahead).wait_recv()
                summed += end_cols[ahead - 1, h]
            end_sum[h] = summed
            give_back(h).start()
        from_inner[...] = jnp.zeros_like(from_inner)

    def deliver(to_row):
        return remote(
            halves.at[to_row % 2],
            landed.at[col],
            end_send.at[to_row],
            end_recv.at[col],
            to_row,
            row,
        )

    for h in range(2):
        summed = total[own_rows(col), h * LANES : (h + 1) * LANES]
        for ahead in range(1, SIDE):
            own_copy(h, ahead).wait_recv()
            summed += from_cols[ahead - 1, h]

        @pl.when(is_end)
        def _():
            give_back(h).wait_recv()

        halves[h] = summed + from_inner[h]
        for to_row in (h, h + 2):

            @pl.when((row != to_row) | (col != to_row))
            def _():
                deliver(to_row).start()

            @pl.when((row == to_row) & (col == to_row))
            def _():
                landed[to_row] = halves[h]

    def delivered(i):
        return remote(
            halves.at[0],
            landed.at[i],
            end_send.at[0],
            end_recv.at[i],
            lax.rem(row + 1, SIDE),
            col,
        )

    energy_of_a = energy_rows_ref[pl.ds(col, 1), :]
    energy_of_b = column_of(energy_rows_ref, row)
    wanted = jnp.bitwise_xor(
        jnp.bitwise_xor(row_label, label_rows_ref[pl.ds(col, 1), :]), occ_ref[batch_size]
    )
    for i in range(SIDE):

        @pl.when((row != col) | (col != i))
        def _():
            delivered(i).wait_recv()

        value = jnp.where(wanted == occ_ref[i], landed[i].T, 0.0)
        out_ref[:, i, :] = value / (
            occ_energy_ref[i] + occ_energy_ref[batch_size] - energy_of_a - energy_of_b
        )

    for h in range(2):
        for ahead in range(1, SIDE):
            own_copy(h, ahead).wait_send()
    for to_row in range(SIDE):

        @pl.when((row != to_row) | (col != to_row))
        def _():
            deliver(to_row).wait_send()

    for distance in range(SIDE - 1):
        for j in range(PIECES):
            for up in (True, False):

                @pl.when(sends(distance, j, up))
                def _():
                    hop(distance, j, up).wait_send()

    @pl.when(is_end)
    def _():
        for j in range(OWN, PIECES):
            give(j).wait_send()

    @pl.when(is_inner)
    def _():
        for h in range(2):
            for ahead in range(1, SIDE):
                end_copy(h, ahead).wait_send()
            give_back(h).wait_send()


def cycle_blocks(
    amplitudes, integrals, occ_irrep, vir_irrep, screen, occ_energy, vir_energy
):
    batch_size, occ_share, vir_share, vir_total = amplitudes.shape
    half = vir_total // 2
    bf16, f32 = jnp.bfloat16, jnp.float32
    given = sum(GIVEN)
    sizes = ((occ_share - given) // OWN,) * OWN + GIVEN
    vmem, smem, dma = pltpu.VMEM, pltpu.SMEM, pltpu.SemaphoreType.DMA
    hops = (2, SIDE - 1, PIECES)
    in_vmem = pl.BlockSpec(memory_space=vmem)
    in_smem = pl.BlockSpec(memory_space=smem)
    anywhere = pl.BlockSpec(memory_space=pl.ANY)
    return pl.pallas_call(
        functools.partial(cycle_kernel, sizes),
        out_shape=jax.ShapeDtypeStruct((LANES, batch_size, LANES), f32),
        in_specs=[in_smem] + [anywhere] * 6,
        out_specs=in_vmem,
        scratch_shapes=[
            smem(occ_irrep.shape, occ_irrep.dtype),
            smem(occ_energy.shape, f32),
            vmem((SIDE, LANES), vir_irrep.dtype),
            vmem((SIDE, LANES), f32),
            dma((4,)),
            vmem((occ_share, vir_share, vir_total), bf16),
            vmem((SIDE, batch_size, occ_share, vir_share, LANES), bf16),
            vmem((SIDE, 8, vir_share, LANES), bf16),
            vmem((8, vir_share, LANES), f32),
            vmem((SIDE, occ_share, vir_share, half), bf16),
            vmem((batch_size * vir_share, half), f32),
            vmem((SIDE - 1, 2, vir_share, LANES), f32),
            vmem((2, vir_share, LANES), f32),
            vmem((SIDE, vir_share, LANES), f32),
            vmem((SIDE, 8, vir_share, LANES), bf16),
            vmem((given, batch_size, vir_share, half), bf16),
            vmem((given, batch_size, vir_share, half), bf16),
            vmem((batch_size * vir_share, half), f32),
            vmem((SIDE - 1, 2, vir_share, LANES), f32),
            vmem((2, vir_share, LANES), f32),
            vmem((2, vir_share, LANES), f32),
            dma((PIECES,)),
            dma((SIDE,)),
            dma(hops),
            dma(hops),
            dma((2, SIDE - 1)),
            dma((2, SIDE - 1)),
            dma((SIDE,)),
            dma((SIDE,)),
            dma((len(GIVEN),)),
            dma((len(GIVEN),)),
            dma((2, SIDE - 1)),
            dma((2, SIDE - 1)),
            dma((2,)),
            dma((2,)),
        ],
        compiler_params=pltpu.CompilerParams(
            collective_id=0, has_side_effects=True, vmem_limit_bytes=64 * 1024 * 1024
        ),
        name="cycle_blocks",
    )(
        screen,
        occ_irrep,
        occ_energy,
        vir_irrep.reshape(SIDE, LANES),
        vir_energy.reshape(SIDE, LANES),
        integrals,
        amplitudes,
    )


def fits_kernel(row_count, column_count, amplitudes):
    batch_size, occ_share, vir_share, vir_total = amplitudes.shape
    return (
        row_count == column_count == batch_size == SIDE
        and vir_share == LANES
        and vir_total == SIDE * LANES
        and occ_share > sum(GIVEN)
        and (occ_share - sum(GIVEN)) % OWN == 0
    )


def on_device(amplitudes, integrals, occ_irrep, vir_irrep, screen, occ_energy, vir_energy):
    row_count = lax.axis_size("row")
    column_count = lax.axis_size("col")
    row, col = lax.axis_index("row"), lax.axis_index("col")
    batch_size, occ_share, vir_share, vir_total = amplitudes.shape
    if fits_kernel(row_count, column_count, amplitudes):
        return cycle_blocks(
            amplitudes, integrals, occ_irrep, vir_irrep, screen, occ_energy, vir_energy
        )
    half = vir_total // 2
    vir_columns = vir_total // column_count
    occ_offset = col * occ_share
    occ_local = lax.dynamic_slice_in_dim(occ_irrep, occ_offset, occ_share)
    vir_local = lax.dynamic_slice_in_dim(vir_irrep, row * vir_share, vir_share)
    screen_rows = lax.dynamic_slice_in_dim(screen, occ_offset, occ_share, 0)
    pair_label = occ_irrep[batch_size]

    folded = folded_integrals(
        integrals, occ_local, vir_local, vir_irrep, screen_rows, pair_label
    )
    gathered = lax.all_gather(folded, "row", axis=1, tiled=True)
    shift = jnp.bitwise_xor(occ_irrep[:batch_size, None], occ_local[None, :])
    keep_amp = (
        jnp.bitwise_xor(shift[:, :, None], vir_local[None, None, :])[:, :, :, None]
        == vir_irrep[None, None, None, :]
    )
    amp_kept = jnp.where(keep_amp, amplitudes, jnp.zeros_like(amplitudes))
    partial = lax.dot_general(
        amp_kept, gathered, (((1, 3), (0, 1)), ((), ())), preferred_element_type=jnp.float32
    )
    whole = lax.all_gather(lax.psum(partial, "col"), "row", axis=1, tiled=True)
    cycle = lax.dynamic_slice_in_dim(whole, col * vir_columns, vir_columns, 1)
    cycle = lax.dynamic_slice_in_dim(cycle, (row * vir_share) % half, vir_share, 2)
    cycle = jnp.transpose(cycle, (2, 0, 1))
    col_irrep = lax.dynamic_slice_in_dim(vir_irrep, col * vir_columns, vir_columns)
    kept = (
        jnp.bitwise_xor(occ_irrep[:batch_size, None], pair_label ^ col_irrep[None, :])[None]
        == vir_local[:, None, None]
    )
    cycle = jnp.where(kept, cycle, 0.0)
    energy_cols = lax.dynamic_slice_in_dim(vir_energy, col * vir_columns, vir_columns)
    energy_rows = lax.dynamic_slice_in_dim(vir_energy, row * vir_share, vir_share)
    denominator = (
        occ_energy[:batch_size][None, :, None]
        + occ_energy[batch_size]
        - energy_cols[None, None, :]
        - energy_rows[:, None, None]
    )
    return cycle / denominator


def solution(mesh):
    in_specs = (
        P("parts", "col", "row", None),
        P(("parts", "col"), "row", None),
        P("parts"),
        P("parts"),
        P("parts", None),
        P("parts"),
        P("parts"),
    )
    out_specs = P("row", "parts", "col")
    return jax.shard_map(
        on_device, mesh=mesh, in_specs=in_specs, out_specs=out_specs, check_vma=False
    )
```
